32 devices in a mesh: ctx: 8 (over y, x, core), head: 4 (over z).
Axes of the slice: x: 2, y: 2, z: 4, core: 2. Of those that a mesh axis runs over, the one named last changes fastest.
Arguments:
- query_input: bfloat16 [8, 512, 4096], P('ctx', 'head'), may hold values from -6 to 6
- key_input: bfloat16 [8, 512, 512], P('ctx', 'head'), may hold values from -6 to 6
- value_input: bfloat16 [8, 512, 512], P('ctx', 'head'), may hold values from -6 to 6
- grad_input: bfloat16 [8, 512, 4096], P('ctx', 'head'), may hold values from -6 to 6
Outputs:
- attended: bfloat16 [8, 512, 4096], P('ctx', 'head')
- query_grad: float32 [8, 512, 4096], P('ctx', 'head')
- key_grad: float32 [8, 512, 512], P('ctx', 'head')
- value_grad: float32 [8, 512, 512], P('ctx', 'head')
The draws below stay inside these ranges and needn't reach their ends.
All inputs are finite; a program needn't handle non-finite values.
Results may differ from the reference program's by a relative error of at most 0.0076.
Values may be sent and summed in bfloat16 or wider, within the bound.
A program may use at most 192 MiB of HBM per device.

```python
import math
import jax
import jax.numpy as jnp
from jax import lax

HD = 128
HEADS = 32
KV_HEADS = 4
STRETCH = 256
BATCH = 2
SEQ = 2048
N_CTX = 8


def block_layout(tensor):
    columns = tensor.shape[-1]
    block_count = SEQ // STRETCH
    return tensor.reshape(BATCH, block_count, STRETCH, columns).transpose(1, 0, 2, 3).reshape(block_count, BATCH * STRETCH, columns)


def draw_query_input(key, part):
    full_shape = (BATCH, SEQ, HEADS, HD)
    base_key = jax.random.fold_in(key, 11)
    sample = jax.random.truncated_normal(base_key, -6.0, 6.0, full_shape, jnp.float32)
    return block_layout(sample.reshape(BATCH, SEQ, HEADS * HD)).astype(jnp.bfloat16)


def draw_key_input(key, part):
    full_shape = (BATCH, SEQ, KV_HEADS, HD)
    base_key = jax.random.fold_in(key, 13)
    sample = jax.random.truncated_normal(base_key, -6.0, 6.0, full_shape, jnp.float32)
    return block_layout(sample.reshape(BATCH, SEQ, KV_HEADS * HD)).astype(jnp.bfloat16)


def block_levels(rng, dims, cuts, low, high):
    level = 1.0
    for dim, parts in cuts:
        steps = jax.random.uniform(jax.random.fold_in(jax.random.fold_in(rng, 6), dim), (parts,), jnp.float32, low / len(cuts), high / len(cuts))
        level = level * jnp.repeat(jnp.exp(steps), dims[dim] // parts).reshape((-1,) + (1,) * (len(dims) - 1 - dim))
    return level


def centred(own_key, extent, spread, most, pieces=(), held_as=jnp.bfloat16):
    drawn = spread * jax.random.normal(own_key, extent, jnp.float32)
    if pieces:
        drawn = drawn * block_levels(own_key, extent, pieces, -0.22, 0.18)
    return jnp.clip(drawn, -most, most).astype(held_as)


def setup_inputs(seed: int = 0) -> dict:
    splits = jax.random.split(jax.random.key(seed), 5)
    return {
        "query_input": draw_query_input(jax.random.fold_in(splits[4], 71), 0),
        "key_input": draw_key_input(jax.random.fold_in(splits[4], 71), 0),
        "value_input": centred(splits[2], (N_CTX, BATCH * STRETCH, KV_HEADS * HD), 1.0, 6.0, ((0, 8), (1, 4))),
        "grad_input": centred(splits[3], (N_CTX, BATCH * STRETCH, HEADS * HD), 1.0, 6.0, ((0, 8), (1, 4))),
    }


def rounded(tensor):
    return lax.optimization_barrier(tensor.astype(jnp.bfloat16)).astype(jnp.float32)

def reference(query_input, key_input, value_input, grad_input):
    sharing = HEADS // KV_HEADS
    scaling = 1.0 / math.sqrt(HD)

    def to_sequences(tensor):
        columns = tensor.shape[-1]
        return tensor.reshape(N_CTX, BATCH, STRETCH, columns).transpose(1, 0, 2, 3).reshape(BATCH, SEQ, columns)

    def to_blocks(tensor):
        columns = tensor.shape[-1]
        return tensor.reshape(BATCH, N_CTX, STRETCH, columns).transpose(1, 0, 2, 3).reshape(N_CTX, BATCH * STRETCH, columns)

    def split_queries(tensor):
        return to_sequences(tensor).reshape(BATCH, SEQ, KV_HEADS, sharing, HD).transpose(0, 2, 3, 1, 4).reshape(BATCH * KV_HEADS, sharing, SEQ, HD)

    def split_pairs(tensor):
        return to_sequences(tensor).reshape(BATCH, SEQ, KV_HEADS, HD).transpose(0, 2, 1, 3).reshape(BATCH * KV_HEADS, SEQ, HD)
    positions = jnp.arange(SEQ, dtype=jnp.int32)
    causal = positions[None, :] <= positions[:, None]

    def single(operands):
        query_part = operands[0].astype(jnp.float32)
        key_part = operands[1].astype(jnp.float32)
        value_part = operands[2].astype(jnp.float32)
        grad_part = operands[3].astype(jnp.float32)
        raw_scores = jnp.einsum('gid,jd->gij', query_part, key_part) * scaling
        scores = jnp.where(causal[None], raw_scores, -jnp.inf)
        highest = lax.optimization_barrier(jnp.max(scores, axis=-1, keepdims=True))
        log_total = highest + jnp.log(lax.optimization_barrier(jnp.sum(jnp.exp(scores - highest), axis=-1, keepdims=True)))
        probs = jnp.exp(scores - log_total)
        weights = rounded(probs)
        attended = jnp.einsum('gij,jd->gid', weights, value_part).astype(jnp.bfloat16)
        attended_back = lax.optimization_barrier(attended).astype(jnp.float32)
        row_dot = lax.optimization_barrier(jnp.sum(grad_part * attended_back, axis=-1, keepdims=True))
        weight_grad = jnp.einsum('gid,jd->gij', grad_part, value_part)
        score_grad = rounded(probs * (weight_grad - row_dot))
        query_grad = scaling * jnp.einsum('gij,jd->gid', score_grad, key_part)
        key_grad = scaling * jnp.einsum('gij,gid->jd', score_grad, query_part)
        value_grad = jnp.einsum('gij,gid->jd', weights, grad_part)
        return (attended, query_grad, key_grad, value_grad)
    attended, query_grad, key_grad, value_grad = lax.map(single, (split_queries(query_input), split_pairs(key_input), split_pairs(value_input), split_queries(grad_input)))

    def merge_queries(tensor):
        return to_blocks(tensor.reshape(BATCH, KV_HEADS, sharing, SEQ, HD).transpose(0, 3, 1, 2, 4).reshape(BATCH, SEQ, HEADS * HD))

    def merge_pairs(tensor):
        return to_blocks(tensor.reshape(BATCH, KV_HEADS, SEQ, HD).transpose(0, 2, 1, 3).reshape(BATCH, SEQ, KV_HEADS * HD))
    return (merge_queries(attended), merge_queries(query_grad), merge_pairs(key_grad), merge_pairs(value_grad))
```

```python
import functools
import math

import jax
import jax.numpy as jnp
from jax import lax
from jax.experimental import pallas as pl
from jax.experimental.pallas import tpu as pltpu
from jax.sharding import PartitionSpec as P

HD = 128
NN = (((1,), (0,)), ((), ()))
F32 = jnp.float32
BF16 = jnp.bfloat16
MESH = pl.DeviceIdType.MESH


def dot(a, b, dims=NN):
    return lax.dot_general(a, b, dims, preferred_element_type=F32)


def pieces_of(size):
    unit = 16
    units = size // unit
    count = min(3, units)
    sizes = [(units // count + (1 if i < units % count else 0)) * unit for i in range(count)]
    starts = [sum(sizes[:i]) for i in range(count)]
    return [slice(a, a + s) for a, s in zip(starts, sizes)]


def orders_of(bits, count):
    links = [d for d in range(bits + 1) if d != bits - 1]
    return [[links[(i + p) % len(links)] for i in range(len(links))] for p in range(count)]


def my_bits(bits):
    block = lax.axis_index("ctx")
    return [block // 2 ** (bits - 1 - d) % 2 for d in range(bits)] + [lax.axis_index("head") % 2]


def partner_of(bits, me, d):
    if d == bits:
        return {"head": lax.axis_index("head") + 1 - 2 * me[d]}
    return {"ctx": lax.axis_index("ctx") + (1 - 2 * me[d]) * 2 ** (bits - 1 - d)}


def greet(bits, me):
    barrier = pltpu.get_barrier_semaphore()
    for d in range(bits + 1):
        pl.semaphore_signal(barrier, inc=1, device_id=partner_of(bits, me, d), device_id_type=MESH)
    pl.semaphore_wait(barrier, bits + 1)


def gather_steps(bits, me, arrays, heads, parts, sems):
    link_send, link_recv, core_send, core_recv = sems
    orders = orders_of(bits, len(parts))
    regions = [list(me) for _ in parts]
    fresh = [list(me) for _ in parts]
    links, cores = [], []

    def copy(ref, index, d, send, recv):
        return pltpu.make_async_remote_copy(
            src_ref=ref.at[index], dst_ref=ref.at[index], send_sem=send, recv_sem=recv,
            device_id=partner_of(bits, me, d), device_id_type=MESH)

    def step(k):
        for c in links:
            c.wait()
        links.clear()
        for p in range(len(parts)):
            if 0 < k <= bits:
                d = orders[p][k - 1]
                fresh[p] = list(regions[p])
                fresh[p][d] = 1 - me[d]
                regions[p][d] = slice(None)
        for p, part in enumerate(parts):
            for a, ref in enumerate(arrays):
                if k < bits:
                    c = copy(ref, (heads, *regions[p], part), orders[p][k], link_send.at[p, k, a], link_recv.at[p, k, a])
                    c.start()
                    links.append(c)
        for p, part in enumerate(parts):
            for a, ref in enumerate(arrays):
                if k <= bits:
                    c = copy(ref, (heads, *fresh[p], part), bits - 1, core_send.at[p, k, a], core_recv.at[p, k, a])
                    c.start()
                    cores.append(c)
        if k > bits:
            for c in cores:
                c.wait()

    return [functools.partial(step, k) for k in range(bits + 2)]


def scatter_steps(bits, me, arrays, outs, h, parts, held, send_sem, recv_sem):
    orders = [[bits - 1] + order[::-1] for order in orders_of(bits, len(parts))]
    now = [[(ref, (part,)) for ref in arrays] for part in parts]
    dims = [list(range(bits + 1)) for _ in parts]
    copies = []

    def pick(p, d, value, tail):
        return (h, *(value if e == d else slice(None) for e in dims[p]), *tail)

    def step(k):
        if k > 0:
            for p, part in enumerate(parts):
                d = orders[p][k - 1]
                for a in range(2):
                    copies[2 * p + a].wait()
                    ref, tail = now[p][a]
                    slot = held[p][k - 1][a]
                    sums = ref[pick(p, d, me[d], tail)].astype(F32) + slot[h].astype(F32)
                    if k > bits:
                        outs[a][part, h * HD:(h + 1) * HD] = sums
                    else:
                        slot[h] = sums.astype(slot.dtype)
                    now[p][a] = (slot, (slice(None),))
                dims[p].remove(d)
            copies.clear()
        if k <= bits:
            for p in range(len(parts)):
                d = orders[p][k]
                for a in range(2):
                    ref, tail = now[p][a]
                    c = pltpu.make_async_remote_copy(
                        src_ref=ref.at[pick(p, d, 1 - me[d], tail)], dst_ref=held[p][k][a].at[h],
                        send_sem=send_sem.at[p, k, a], recv_sem=recv_sem.at[p, k, a],
                        device_id=partner_of(bits, me, d), device_id_type=MESH)
                    c.start()
                    copies.append(c)

    return [functools.partial(step, k) for k in range(bits + 2)]


def layer_kernel(bits, sharing, q_ref, g_ref, k_ref, v_ref, o_ref, dq_ref, ok_ref, ov_ref,
                 ka, va, dka, dva, s_scr, p_scr, qin, gin, ost, dqst, kst, vst, qm, gm, om, dm, din,
                 ds_scr, qt, gt, qn, gn, acc, top, total, drow,
                 swap_send, swap_recv, own_sem, in_sem, out_sem,
                 link_send, link_recv, core_send, core_recv, send_sem, recv_sem, *slots):
    rows, pair_width = k_ref.shape
    pairs = pair_width // HD
    block = lax.axis_index("ctx")
    half = lax.axis_index("head") % 2
    span = 2 * rows
    wide = rows * sharing
    cols_of = sharing * HD
    step_cols = 2 * rows
    scaling = 1.0 / math.sqrt(HD)
    factor = scaling * math.log2(math.e)
    me = my_bits(bits)
    slot_list = iter(slots)
    gather_parts = pieces_of(rows)
    scatter_parts = gather_parts
    held = [[[next(slot_list) for _ in range(2)] for _ in range(bits + 1)] for _ in scatter_parts]
    count = 2 ** bits
    light = block < count // 2
    last = pairs - 1

    own = [pltpu.make_async_copy(src.at[:, h * HD:(h + 1) * HD], dst.at[(h, *me)], own_sem.at[h, a])
           for h in range(pairs) for a, (src, dst) in enumerate(((k_ref, ka), (v_ref, va)))]
    loads = [[pltpu.make_async_copy(src.at[:, h * cols_of:(h + 1) * cols_of], dst.at[h], in_sem.at[h, a])
              for a, (src, dst) in enumerate(((q_ref, qin), (g_ref, gin)))] for h in range(pairs)]
    stores = [[pltpu.make_async_copy(src.at[h], dst.at[:, h * cols_of:(h + 1) * cols_of], out_sem.at[h, a])
               for a, (src, dst) in enumerate(((ost, o_ref), (dqst, dq_ref)))] for h in range(pairs)]
    for c in own:
        c.start()
    for pair in loads:
        for c in pair:
            c.start()
    greet(bits, me)
    for c in own:
        c.wait()

    groups = [slice(0, 1)] + ([slice(1, pairs)] if pairs > 1 else [])
    gathers = [gather_steps(bits, me, (ka, va), heads, gather_parts,
                            [r.at[i] for r in (link_send, link_recv, core_send, core_recv)])
               for i, heads in enumerate(groups)]
    pending = []

    def advance(work):
        if work:
            work.pop(0)()

    def drain(work):
        while work:
            work.pop(0)()

    def keys_at(b, many):
        return pl.ds(pl.multiple_of(b * span, span), many * span)

    def bits_of(b, many=1):
        ctx = tuple(b // 2 ** (bits - 1 - d) % 2 for d in range(bits))
        return ctx if many == 1 else ctx[:-1]

    def load(ref, g, b, many):
        return ref[(g, *bits_of(b, many))].reshape(many * span, HD)

    def each(first, stop, body):
        @pl.loop(0, stop // 2)
        def _(i):
            body(2 * i, 2)

        @pl.when(stop % 2 == 1)
        def _():
            body(stop - 1, 1)

    def swap(i, src, dst):
        return pltpu.make_async_remote_copy(
            src_ref=src, dst_ref=dst, send_sem=swap_send.at[i], recv_sem=swap_recv.at[i],
            device_id=partner_of(bits, me, 0), device_id_type=MESH)

    lend = [swap(0, qin.at[last], qm), swap(1, gin.at[last], gm)]
    give = [swap(2, om, ost.at[last]), swap(3, dm, din)]

    def clear(g, first):
        for ref in (dka, dva):
            @pl.loop(first, count)
            def _(b):
                ref[(g, *bits_of(b))] = jnp.zeros((2, rows, HD), ref.dtype)

    def prepare(q_src, g_src):
        for h in range(sharing):
            part = slice(h * rows, (h + 1) * rows)
            qt[:, part] = q_src[:, h * HD:(h + 1) * HD].T
            gt[:, part] = g_src[:, h * HD:(h + 1) * HD].T
        top[...] = jnp.full_like(top, -jnp.inf)

    def attend(g, block, out_ref, dq_out, again, polls):
        def poll():
            if polls:
                polls.pop(0)()

        def scores(b, many, masked=False):
            kb = load(ka, g, b, many)
            for c in range(0, wide, step_cols):
                cols = slice(c, c + step_cols)
                s = dot(kb, qt[:, cols])
                if masked:
                    key_pos = lax.broadcasted_iota(jnp.int32, s.shape, 0)
                    row_pos = half * rows + lax.broadcasted_iota(jnp.int32, s.shape, 1) % rows
                    s = jnp.where(key_pos <= row_pos, s, -jnp.inf)
                s_scr[keys_at(b, many), cols] = s
                top[:, cols] = jnp.maximum(top[:, cols], s.reshape(many * span // 8, 8, step_cols).max(axis=0))

        each(0, block, scores)
        scores(block, 1, True)
        poll()
        highest = jnp.max(top[...], axis=0, keepdims=True) * factor
        total[...] = jnp.zeros_like(total)
        acc[...] = jnp.zeros_like(acc)

        def weigh(b, many):
            vt = load(va, g, b, many).T
            for c in range(0, wide, step_cols):
                cols = slice(c, c + step_cols)
                p = jnp.exp2(s_scr[keys_at(b, many), cols] * factor - highest[:, cols])
                total[:, cols] += p.reshape(many * span // 8, 8, step_cols).sum(axis=0)
                pb = p.astype(BF16)
                p_scr[keys_at(b, many), cols] = pb
                acc[:, cols] += dot(vt, pb)

        each(0, block + 1, weigh)
        poll()
        inverse = 1.0 / jnp.sum(total[...], axis=0, keepdims=True)
        for h in range(sharing):
            part = slice(h * rows, (h + 1) * rows)
            inv = inverse[:, part]
            out = (acc[:, part] * inv).astype(BF16)
            out_ref[:, h * HD:(h + 1) * HD] = out.T
            grad = gt[:, part].astype(F32)
            drow[:, part] = jnp.sum(grad * out.astype(F32), axis=0, keepdims=True)
            gn[part, :] = (grad * inv).astype(BF16).T
            qn[part, :] = (qt[:, part].astype(F32) * (inv * scaling)).astype(BF16).T
        acc[...] = jnp.zeros_like(acc)

        def back(b, many):
            keys = slice(0, many * span)
            kt = load(ka, g, b, many).T
            vb = load(va, g, b, many)
            for c in range(0, wide, step_cols):
                cols = slice(c, c + step_cols)
                dp = dot(vb, gt[:, cols])
                pb = p_scr[keys_at(b, many), cols]
                ds_scr[keys, cols] = (pb.astype(F32) * (dp - drow[:, cols])).astype(BF16)
            dk = dot(ds_scr[keys, :], qn[...])
            dv = dot(p_scr[keys_at(b, many), :], gn[...])
            for c in range(0, wide, step_cols):
                cols = slice(c, c + step_cols)
                acc[:, cols] += dot(kt, ds_scr[keys, cols])
            for ref, add in ((dka, dk), (dva, dv)):
                where = (g, *bits_of(b, many))
                if again:
                    add = add + load(ref, g, b, many).astype(F32)
                ref[where] = add.astype(ref.dtype).reshape(ref[where].shape)

        each(0, block + 1, back)
        poll()
        for h in range(sharing):
            part = slice(h * rows, (h + 1) * rows)
            dq = acc[:, part] * (inverse[:, part] * scaling)
            dq_out[:, h * HD:(h + 1) * HD] = dq.T.astype(dq_out.dtype)

    def started(g):
        work = scatter_steps(bits, me, (dka, dva), (kst, vst), g, scatter_parts, held, send_sem.at[g], recv_sem.at[g])
        work.pop(0)()
        return work

    advance(gathers[0])
    if len(gathers) > 1:
        advance(gathers[1])
    for c in loads[0]:
        c.wait()
    prepare(qin.at[0], gin.at[0])
    for g in range(last):
        clear(g, block + 1)
    clear(last, jnp.where(light, block + 1, 0))
    for _ in range(bits - 1):
        for work in gathers:
            advance(work)
    for pair in loads[1:]:
        for c in pair:
            c.wait()

    @pl.when(~light)
    def _():
        for c in lend:
            c.start()
    drain(gathers[0])

    scatters = []
    for g in range(last):
        if g > 0:
            prepare(qin.at[g], gin.at[g])
            drain(gathers[1])
        polls = []
        if g == 0:
            polls = [lambda: advance(gathers[1])]
        elif g > 1 or g == last - 1:
            work = scatters[0] if scatters else []
            polls = [functools.partial(advance, work)] * 3
        attend(g, block, ost.at[g], dqst.at[g], False, polls)
        for c in stores[g]:
            c.start()
        scatters.append(started(g))
    tail = scatters

    @pl.when(light)
    def _():
        prepare(qin.at[last], gin.at[last])
        attend(last, block, ost.at[last], dqst.at[last], False, [])
        for c in stores[last]:
            c.start()
        for c in lend:
            c.wait_recv()
        prepare(qm, gm)
        attend(last, block + count // 2, om, dm, True, [])
        for c in give:
            c.start()

    tail.append(started(last))
    while any(tail):
        for work in tail:
            advance(work)

    outs = [pltpu.make_async_copy(src, dst, out_sem.at[pairs, a]) for a, (src, dst) in enumerate(((kst, ok_ref), (vst, ov_ref)))]
    for c in outs:
        c.start()

    @pl.when(light)
    def _():
        for c in give:
            c.wait_send()

    @pl.when(~light)
    def _():
        for c in lend:
            c.wait_send()
        for c in give:
            c.wait_recv()
        dqst[last] = din[...].astype(F32)
        for c in stores[last]:
            c.start()

    for pair in stores:
        for c in pair:
            c.wait()
    for c in outs:
        c.wait()


def layer(bits, q, g, k, v):
    rows, width = q.shape
    pair_width = k.shape[1]
    pairs = pair_width // HD
    sharing = width // pair_width
    wide = rows * sharing
    seq = 2 ** (bits + 1) * rows
    count = len(pieces_of(rows))
    parts = pieces_of(rows)
    anyspace = pl.BlockSpec(memory_space=pl.ANY)
    whole = pltpu.VMEM((pairs,) + (2,) * (bits + 1) + (rows, HD), BF16)
    sem = pltpu.SemaphoreType.DMA
    slots = [pltpu.VMEM((pairs,) + (2,) * (bits - k) + (part.stop - part.start, HD), BF16)
             for part in parts for k in range(bits + 1) for _ in range(2)]
    head = (rows, sharing * HD)
    return pl.pallas_call(
        functools.partial(layer_kernel, bits, sharing),
        out_shape=(
            jax.ShapeDtypeStruct((rows, width), BF16),
            jax.ShapeDtypeStruct((rows, width), F32),
            jax.ShapeDtypeStruct((rows, pair_width), F32),
            jax.ShapeDtypeStruct((rows, pair_width), F32),
        ),
        in_specs=[anyspace] * 4,
        out_specs=(anyspace,) * 4,
        scratch_shapes=[
            whole, whole, whole, whole,
            pltpu.VMEM((seq, wide), F32),
            pltpu.VMEM((seq, wide), BF16),
            pltpu.VMEM((pairs,) + head, BF16),
            pltpu.VMEM((pairs,) + head, BF16),
            pltpu.VMEM((pairs,) + head, BF16),
            pltpu.VMEM((pairs,) + head, F32),
            pltpu.VMEM((rows, pair_width), F32),
            pltpu.VMEM((rows, pair_width), F32),
            *[pltpu.VMEM(head, BF16) for _ in range(5)],
            pltpu.VMEM((4 * rows, wide), BF16),
            *[pltpu.VMEM((HD, wide), BF16) for _ in range(2)],
            *[pltpu.VMEM((wide, HD), BF16) for _ in range(2)],
            pltpu.VMEM((HD, wide), F32),
            pltpu.VMEM((8, wide), F32),
            pltpu.VMEM((8, wide), F32),
            pltpu.VMEM((1, wide), F32),
            sem((4,)),
            sem((4,)),
            sem((pairs, 2)),
            sem((pairs, 2)),
            sem((pairs + 1, 2)),
            sem((2, count, bits, 2)),
            sem((2, count, bits, 2)),
            sem((2, count, bits + 1, 2)),
            sem((2, count, bits + 1, 2)),
            sem((pairs, len(parts), bits + 1, 2)),
            sem((pairs, len(parts), bits + 1, 2)),
        ] + slots,
        compiler_params=pltpu.CompilerParams(collective_id=0, has_side_effects=True, vmem_limit_bytes=63 * 2**20),
        name="layer",
    )(q, g, k, v)


def on_device(query_input, key_input, value_input, grad_input):
    bits = (lax.axis_size("ctx") - 1).bit_length()
    outs = layer(bits, query_input[0], grad_input[0], key_input[0], value_input[0])
    return tuple(out[None] for out in outs)


def solution(mesh):
    spec = P("ctx", "head", None)
    return jax.shard_map(on_device, mesh=mesh, in_specs=(spec,) * 4, out_specs=(spec,) * 4, check_vma=False)
```

```python
import functools
import math

import jax
import jax.numpy as jnp
from jax import lax
from jax.experimental import pallas as pl
from jax.experimental.pallas import tpu as pltpu
from jax.sharding import PartitionSpec as P

HD = 128
NN = (((1,), (0,)), ((), ()))
F32 = jnp.float32
BF16 = jnp.bfloat16
MESH = pl.DeviceIdType.MESH


def dot(a, b, dims=NN):
    return lax.dot_general(a, b, dims, preferred_element_type=F32)


def pieces_of(size):
    unit = 16
    units = size // unit
    count = min(3, units)
    sizes = [(units // count + (1 if i < units % count else 0)) * unit for i in range(count)]
    starts = [sum(sizes[:i]) for i in range(count)]
    return [slice(a, a + s) for a, s in zip(starts, sizes)]


def orders_of(bits, count):
    links = [d for d in range(bits + 1) if d != bits - 1]
    return [[links[(i + p) % len(links)] for i in range(len(links))] for p in range(count)]


def my_bits(bits):
    block = lax.axis_index("ctx")
    return [block // 2 ** (bits - 1 - d) % 2 for d in range(bits)] + [lax.axis_index("head") % 2]


def partner_of(bits, me, d):
    if d == bits:
        return {"head": lax.axis_index("head") + 1 - 2 * me[d]}
    return {"ctx": lax.axis_index("ctx") + (1 - 2 * me[d]) * 2 ** (bits - 1 - d)}


def greet(bits, me):
    barrier = pltpu.get_barrier_semaphore()
    for d in range(bits + 1):
        pl.semaphore_signal(barrier, inc=1, device_id=partner_of(bits, me, d), device_id_type=MESH)
    pl.semaphore_wait(barrier, bits + 1)


def gather_steps(bits, me, arrays, heads, parts, send_sem, recv_sem):
    orders = orders_of(bits, len(parts))
    regions = [list(me) for _ in parts]
    for region in regions:
        region[bits - 1] = slice(None)
    copies = []

    def step(k):
        for c in copies:
            c.wait()
        copies.clear()
        for p, part in enumerate(parts):
            if k > 0:
                regions[p][orders[p][k - 1]] = slice(None)
            if k < bits:
                for a, ref in enumerate(arrays):
                    index = (heads, *regions[p], part)
                    c = pltpu.make_async_remote_copy(
                        src_ref=ref.at[index], dst_ref=ref.at[index],
                        send_sem=send_sem.at[p, k, a], recv_sem=recv_sem.at[p, k, a],
                        device_id=partner_of(bits, me, orders[p][k]), device_id_type=MESH)
                    c.start()
                    copies.append(c)

    return [functools.partial(step, k) for k in range(bits + 1)]


def scatter_steps(bits, me, arrays, outs, arrived, h, mine, theirs, parts, held, send_sem, recv_sem):
    core = bits - 1
    orders = [order[::-1] for order in orders_of(bits, len(parts))]
    now = [[(ref, (part,)) for ref in arrays] for part in parts]
    dims = [list(range(bits + 1)) for _ in parts]
    copies = []

    def pick(p, d, value, tail):
        return (h, *(value if e == d else slice(None) for e in dims[p]), *tail)

    def send(p, k, a, src, dst, d):
        c = pltpu.make_async_remote_copy(
            src_ref=src, dst_ref=dst, send_sem=send_sem.at[p, k, a], recv_sem=recv_sem.at[p, k, a],
            device_id=partner_of(bits, me, d), device_id_type=MESH)
        c.start()
        copies.append(c)

    def step(k):
        ready = list(copies)
        copies.clear()
        if k > bits:
            for c in ready:
                c.wait()
            for a in range(2):
                outs[a][:, theirs] = arrived[a][h].astype(F32)
            return
        for p, part in enumerate(parts):
            for a in range(2):
                if k > 0:
                    d = orders[p][k - 1]
                    ready[2 * p + a].wait()
                    ref, tail = now[p][a]
                    slot = held[p][k - 1][a]
                    sums = ref[pick(p, d, me[d], tail)].astype(F32) + slot[h].astype(F32)
                    slot[h] = sums.astype(slot.dtype)
                    now[p][a] = (slot, (slice(None),))
                if k == bits:
                    outs[a][part, mine] = jnp.where(me[core] == 0, sums[0], sums[1])
                    send(p, k, a, slot.at[h, 1 - me[core]], arrived[a].at[h, part], core)
            if k > 0:
                dims[p].remove(orders[p][k - 1])
            if k < bits:
                d = orders[p][k]
                for a in range(2):
                    ref, tail = now[p][a]
                    send(p, k, a, ref.at[pick(p, d, 1 - me[d], tail)], held[p][k][a].at[h], d)

    return [functools.partial(step, k) for k in range(bits + 2)]


def layer_kernel(bits, sharing, q_ref, g_ref, k_ref, v_ref, o_ref, dq_ref, ok_ref, ov_ref,
                 ka, va, dka, dva, s_scr, p_scr, qin, gin, ost, dqst, qm, gm, om, dm, kst, vst, kin, vin,
                 ds_scr, qt, gt, qn, gn, acc, top, total, drow,
                 own_sem, pass_send, pass_recv, in_sem, swap_send, swap_recv, out_sem, back_send, back_recv,
                 lend_send, lend_recv, final_sem, gather_send, gather_recv, send_sem, recv_sem, *slots):
    rows, pair_width = k_ref.shape
    pairs = pair_width // HD
    heads = pairs // 2
    last = heads - 1
    core = bits - 1
    block = lax.axis_index("ctx")
    half = lax.axis_index("head") % 2
    span = 2 * rows
    wide = rows * sharing
    step_cols = 2 * rows
    scaling = 1.0 / math.sqrt(HD)
    factor = scaling * math.log2(math.e)
    me = my_bits(bits)
    slot_list = iter(slots)
    parts = pieces_of(rows)
    held = [[[next(slot_list) for _ in range(2)] for _ in range(bits)] for _ in parts]
    count = 2 ** bits
    light = block < count // 2
    beside = block + 1 - 2 * me[core]

    def columns(side, h, width):
        return pl.ds(pl.multiple_of((side * heads + h) * width, width), width)

    def local(src, dst, sem):
        return pltpu.make_async_copy(src, dst, sem)

    def remote(src, dst, send, recv, d):
        return pltpu.make_async_remote_copy(
            src_ref=src, dst_ref=dst, send_sem=send, recv_sem=recv,
            device_id=partner_of(bits, me, d), device_id_type=MESH)

    head_cols = sharing * HD
    pair_refs = ((k_ref, ka), (v_ref, va))
    row_refs = ((q_ref, qin), (g_ref, gin))
    out_refs = ((ost, o_ref), (dqst, dq_ref))
    own = [[local(src.at[:, columns(me[core], h, HD)], dst.at[(h, *me)], own_sem.at[h, a])
            for a, (src, dst) in enumerate(pair_refs)] for h in range(heads)]
    passed = [[remote(src.at[:, columns(1 - me[core], h, HD)], dst.at[(h, *me)], pass_send.at[h, a], pass_recv.at[h, a], core)
               for a, (src, dst) in enumerate(pair_refs)] for h in range(heads)]
    loads = [[local(src.at[:, columns(me[core], h, head_cols)], dst.at[0, h], in_sem.at[h, a])
              for a, (src, dst) in enumerate(row_refs)] for h in range(heads)]
    swaps = [[remote(src.at[:, columns(1 - me[core], h, head_cols)], dst.at[1, h], swap_send.at[h, a], swap_recv.at[h, a], core)
              for a, (src, dst) in enumerate(row_refs)] for h in range(heads)]
    stores = [[local(src.at[0, h], dst.at[:, columns(me[core], h, head_cols)], out_sem.at[h, a])
               for a, (src, dst) in enumerate(out_refs)] for h in range(heads)]
    backs = [[remote(src.at[1, h], dst.at[:, columns(me[core], h, head_cols)], back_send.at[h, a], back_recv.at[h, a], core)
              for a, (src, dst) in enumerate(out_refs)] for h in range(heads)]
    lend = [remote(src.at[:, columns(me[core], last, head_cols)], dst, lend_send.at[a], lend_recv.at[a], 0)
            for a, (src, dst) in enumerate(((q_ref, qm), (g_ref, gm)))]
    give = [remote(src, dst.at[:, columns(me[core], last, head_cols)], lend_send.at[2 + a], lend_recv.at[2 + a], 0)
            for a, (src, dst) in enumerate(((om, o_ref), (dm, dq_ref)))]

    def start(copies):
        for c in copies:
            c.start()

    def wait(copies):
        for c in copies:
            c.wait()

    for h in range(heads):
        start(own[h])
    start(loads[0])
    greet(bits, me)
    for h in range(heads):
        start(passed[h])
    start(swaps[0])

    @pl.when(light)
    def _():
        for h in range(1, heads):
            start(loads[h])

    for h in range(1, heads):
        start(swaps[h])

    first_k = gather_steps(bits, me, (ka,), 0, parts, gather_send.at[0], gather_recv.at[0])
    first_v = gather_steps(bits, me, (va,), 0, parts, gather_send.at[1], gather_recv.at[1])
    rest = gather_steps(bits, me, (ka, va), slice(1, heads), parts, gather_send.at[2], gather_recv.at[2])

    def advance(work):
        if work:
            work.pop(0)()

    def drain(work):
        while work:
            work.pop(0)()

    def keys_at(b, many):
        return pl.ds(pl.multiple_of(b * span, span), many * span)

    def bits_of(b, many=1):
        ctx = tuple(b // 2 ** (bits - 1 - d) % 2 for d in range(bits))
        return ctx if many == 1 else ctx[:-1]

    def load(ref, g, b, many):
        return ref[(g, *bits_of(b, many))].reshape(many * span, HD)

    def each(first, stop, body):
        @pl.loop(0, stop // 2)
        def _(i):
            body(2 * i, 2)

        @pl.when(stop % 2 == 1)
        def _():
            body(stop - 1, 1)

    def clear(g, first):
        for ref in (dka, dva):
            @pl.loop(first, count)
            def _(b):
                ref[(g, *bits_of(b))] = jnp.zeros((2, rows, HD), ref.dtype)

    def prepare(q_src, g_src):
        for h in range(sharing):
            part = slice(h * rows, (h + 1) * rows)
            qt[:, part] = q_src[:, h * HD:(h + 1) * HD].T
            gt[:, part] = g_src[:, h * HD:(h + 1) * HD].T
        top[...] = jnp.full_like(top, -jnp.inf)

    def attend(g, block, out_ref, dq_out, again, polls):
        def poll():
            if polls:
                polls.pop(0)()

        def scores(b, many, masked=False):
            kb = load(ka, g, b, many)
            for c in range(0, wide, step_cols):
                cols = slice(c, c + step_cols)
                s = dot(kb, qt[:, cols])
                if masked:
                    key_pos = lax.broadcasted_iota(jnp.int32, s.shape, 0)
                    row_pos = half * rows + lax.broadcasted_iota(jnp.int32, s.shape, 1) % rows
                    s = jnp.where(key_pos <= row_pos, s, -jnp.inf)
                s_scr[keys_at(b, many), cols] = s
                top[:, cols] = jnp.maximum(top[:, cols], s.reshape(many * span // 8, 8, step_cols).max(axis=0))

        each(0, block, scores)
        scores(block, 1, True)
        poll()
        highest = jnp.max(top[...], axis=0, keepdims=True) * factor
        total[...] = jnp.zeros_like(total)
        acc[...] = jnp.zeros_like(acc)

        def weigh(b, many):
            vt = load(va, g, b, many).T
            for c in range(0, wide, step_cols):
                cols = slice(c, c + step_cols)
                p = jnp.exp2(s_scr[keys_at(b, many), cols] * factor - highest[:, cols])
                total[:, cols] += p.reshape(many * span // 8, 8, step_cols).sum(axis=0)
                pb = p.astype(BF16)
                p_scr[keys_at(b, many), cols] = pb
                acc[:, cols] += dot(vt, pb)

        each(0, block + 1, weigh)
        poll()
        inverse = 1.0 / jnp.sum(total[...], axis=0, keepdims=True)
        for h in range(sharing):
            part = slice(h * rows, (h + 1) * rows)
            inv = inverse[:, part]
            out = (acc[:, part] * inv).astype(BF16)
            out_ref[:, h * HD:(h + 1) * HD] = out.T
            grad = gt[:, part].astype(F32)
            drow[:, part] = jnp.sum(grad * out.astype(F32), axis=0, keepdims=True)
            gn[part, :] = (grad * inv).astype(BF16).T
            qn[part, :] = (qt[:, part].astype(F32) * (inv * scaling)).astype(BF16).T
        acc[...] = jnp.zeros_like(acc)

        def back(b, many):
            keys = slice(0, many * span)
            kt = load(ka, g, b, many).T
            vb = load(va, g, b, many)
            for c in range(0, wide, step_cols):
                cols = slice(c, c + step_cols)
                dp = dot(vb, gt[:, cols])
                pb = p_scr[keys_at(b, many), cols]
                ds_scr[keys, cols] = (pb.astype(F32) * (dp - drow[:, cols])).astype(BF16)
            dk = dot(ds_scr[keys, :], qn[...])
            dv = dot(p_scr[keys_at(b, many), :], gn[...])
            for c in range(0, wide, step_cols):
                cols = slice(c, c + step_cols)
                acc[:, cols] += dot(kt, ds_scr[keys, cols])
            for ref, add in ((dka, dk), (dva, dv)):
                where = (g, *bits_of(b, many))
                if again:
                    add = add + load(ref, g, b, many).astype(F32)
                ref[where] = add.astype(ref.dtype).reshape(ref[where].shape)

        each(0, block + 1, back)
        poll()
        for h in range(sharing):
            part = slice(h * rows, (h + 1) * rows)
            dq = (acc[:, part] * (inverse[:, part] * scaling)).astype(dq_out.dtype)
            dq_out[:, h * HD:(h + 1) * HD] = dq.T

    def scatter(h):
        return scatter_steps(bits, me, (dka, dva), (kst, vst), (kin, vin), h, columns(me[core], h, HD),
                             columns(1 - me[core], h, HD), parts, held, send_sem.at[h], recv_sem.at[h])

    wait(own[0])
    wait(passed[0])
    advance(first_k)
    advance(first_v)
    wait(loads[0])
    prepare(qin.at[0, 0], gin.at[0, 0])
    for h in range(last):
        clear(h, block + 1)
    clear(last, jnp.where(light, block + 1, 0))
    advance(first_k)
    advance(first_v)
    for h in range(1, heads):
        wait(own[h])
        wait(passed[h])
    advance(rest)
    for k in range(2, bits):
        advance(first_k)
        advance(first_v)
        advance(rest)
    drain(first_k)

    pending = []
    for h in range(last):
        polls = [lambda: drain(first_v), lambda: advance(rest), lambda: None]
        if h > 0:
            drain(rest)
            wait(loads[h])
            prepare(qin.at[0, h], gin.at[0, h])
            polls = []
        attend(h, block, ost.at[0, h], dqst.at[0, h], False, polls)
        start(stores[h])
        if h == 0:
            @pl.when(~light)
            def _():
                start(lend)
        wait(swaps[h])
        prepare(qin.at[1, h], gin.at[1, h])
        attend(h, beside, ost.at[1, h], dqst.at[1, h], True, [])
        start(backs[h])
        work = scatter(h)
        advance(work)
        pending.append(work)
    drain(rest)
    wait(swaps[last])

    @pl.when(light)
    def _():
        wait(loads[last])
        prepare(qin.at[0, last], gin.at[0, last])
        attend(last, block, ost.at[0, last], dqst.at[0, last], False, [])
        start(stores[last])
        for c in lend:
            c.wait_recv()
        prepare(qm, gm)
        attend(last, block + count // 2, om, dm, True, [])
        start(give)

    def step():
        for work in pending:
            advance(work)

    prepare(qin.at[1, last], gin.at[1, last])
    attend(last, beside, ost.at[1, last], dqst.at[1, last], True, [lambda: None, step, step])
    start(backs[last])
    pending.append(scatter(last))
    while any(pending):
        step()
    finals = [local(src, dst, final_sem.at[a]) for a, (src, dst) in enumerate(((kst, ok_ref), (vst, ov_ref)))]
    start(finals)

    @pl.when(light)
    def _():
        wait(stores[last])
        for c in give:
            c.wait_send()

    @pl.when(~light)
    def _():
        for c in lend:
            c.wait_send()
        for c in give:
            c.wait_recv()

    for h in range(last):
        wait(stores[h])
    for h in range(heads):
        wait(backs[h])
    wait(finals)


def layer(bits, q, g, k, v):
    rows, width = q.shape
    pair_width = k.shape[1]
    pairs = pair_width // HD
    sharing = width // pair_width
    wide = rows * sharing
    seq = 2 ** (bits + 1) * rows
    heads = pairs // 2
    parts = pieces_of(rows)
    count = len(parts)
    anyspace = pl.BlockSpec(memory_space=pl.ANY)
    whole = pltpu.VMEM((heads,) + (2,) * (bits + 1) + (rows, HD), BF16)
    sem = pltpu.SemaphoreType.DMA
    slots = [pltpu.VMEM((heads,) + (2,) * (bits - k) + (part.stop - part.start, HD), BF16)
             for part in parts for k in range(bits) for _ in range(2)]
    head = (rows, sharing * HD)
    return pl.pallas_call(
        functools.partial(layer_kernel, bits, sharing),
        out_shape=(
            jax.ShapeDtypeStruct((rows, width), BF16),
            jax.ShapeDtypeStruct((rows, width), BF16),
            jax.ShapeDtypeStruct((rows, pair_width), F32),
            jax.ShapeDtypeStruct((rows, pair_width), F32),
        ),
        in_specs=[anyspace] * 4,
        out_specs=(anyspace,) * 4,
        scratch_shapes=[
            whole, whole, whole, whole,
            pltpu.VMEM((seq, wide), F32),
            pltpu.VMEM((seq, wide), BF16),
            *[pltpu.VMEM((2, heads) + head, BF16) for _ in range(4)],
            *[pltpu.VMEM(head, BF16) for _ in range(4)],
            *[pltpu.VMEM((rows, pair_width), F32) for _ in range(2)],
            *[pltpu.VMEM((heads, rows, HD), BF16) for _ in range(2)],
            pltpu.VMEM((4 * rows, wide), BF16),
            *[pltpu.VMEM((HD, wide), BF16) for _ in range(2)],
            *[pltpu.VMEM((wide, HD), BF16) for _ in range(2)],
            pltpu.VMEM((HD, wide), F32),
            pltpu.VMEM((8, wide), F32),
            pltpu.VMEM((8, wide), F32),
            pltpu.VMEM((1, wide), F32),
            *[sem((heads, 2)) for _ in range(9)],
            sem((4,)),
            sem((4,)),
            sem((2,)),
            *[sem((3, count, bits, 2)) for _ in range(2)],
            *[sem((heads, count, bits + 1, 2)) for _ in range(2)],
        ] + slots,
        compiler_params=pltpu.CompilerParams(collective_id=0, has_side_effects=True, vmem_limit_bytes=63 * 2**20),
        name="layer",
    )(q, g, k, v)


def on_device(query_input, key_input, value_input, grad_input):
    bits = (lax.axis_size("ctx") - 1).bit_length()
    outs = layer(bits, query_input[0], grad_input[0], key_input[0], value_input[0])
    return tuple(out[None].astype(F32 if i else BF16) for i, out in enumerate(outs))


def solution(mesh):
    spec = P("ctx", "head", None)
    return jax.shard_map(on_device, mesh=mesh, in_specs=(spec,) * 4, out_specs=(spec,) * 4, check_vma=False)
```

```python
import functools
import math

import jax
import jax.numpy as jnp
from jax import lax
from jax.experimental import pallas as pl
from jax.experimental.pallas import tpu as pltpu
from jax.sharding import PartitionSpec as P

HD = 128
NN = (((1,), (0,)), ((), ()))
F32 = jnp.float32
BF16 = jnp.bfloat16
MESH = pl.DeviceIdType.MESH


def dot(a, b, dims=NN):
    return lax.dot_general(a, b, dims, preferred_element_type=F32)


def pieces_of(size):
    unit = 16
    units = size // unit
    count = min(3, units)
    sizes = [(units // count + (1 if i < units % count else 0)) * unit for i in range(count)]
    starts = [sum(sizes[:i]) for i in range(count)]
    return [slice(a, a + s) for a, s in zip(starts, sizes)]


def orders_of(bits, count):
    links = [d for d in range(bits + 1) if d != bits - 1]
    return [[links[(i + p) % len(links)] for i in range(len(links))] for p in range(count)]


def my_bits(bits):
    block = lax.axis_index("ctx")
    return [block // 2 ** (bits - 1 - d) % 2 for d in range(bits)] + [lax.axis_index("head") % 2]


def partner_of(bits, me, d):
    if d == bits:
        return {"head": lax.axis_index("head") + 1 - 2 * me[d]}
    return {"ctx": lax.axis_index("ctx") + (1 - 2 * me[d]) * 2 ** (bits - 1 - d)}


def greet(bits, me):
    barrier = pltpu.get_barrier_semaphore()
    for d in range(bits + 1):
        pl.semaphore_signal(barrier, inc=1, device_id=partner_of(bits, me, d), device_id_type=MESH)
    pl.semaphore_wait(barrier, bits + 1)


def gather_steps(bits, me, light, arrays, heads, causal, parts, send_sem, recv_sem):
    orders = orders_of(bits, len(parts))
    started = []

    def copies_at(p, k, top):
        region = list(me)
        region[bits - 1] = slice(None)
        for d in orders[p][:k]:
            region[d] = slice(None)
        if not top:
            region[0] = me[0]
        index = (heads, *region, parts[p])
        return [pltpu.make_async_remote_copy(
            src_ref=ref.at[index], dst_ref=ref.at[index],
            send_sem=send_sem.at[p, k, a], recv_sem=recv_sem.at[p, k, a],
            device_id=partner_of(bits, me, orders[p][k]), device_id_type=MESH) for a, ref in enumerate(arrays)]

    def step(k):
        for act in started:
            act()
        started.clear()
        if k == bits:
            return
        low, high = [], []
        for p in range(len(parts)):
            done = orders[p][:k]
            full = copies_at(p, k, True)
            if causal and orders[p][k] == 0:
                low.append(("send", full))
                high.append(("recv", full))
            elif causal and 0 in done:
                low.append(("both", copies_at(p, k, False)))
                high.append(("both", full))
            else:
                for c in full:
                    c.start()
                low.append(("wait", full))
                high.append(("wait", full))
        sides = ((light, low), (~light, high))
        for side, work in sides:
            sent = [c for kind, group in work if kind in ("send", "both") for c in group]
            if sent:
                @pl.when(side)
                def _():
                    for c in sent:
                        c.start()

        def finish():
            if all(kind == "wait" for kind, _ in low):
                for _, group in low:
                    for c in group:
                        c.wait()
                return
            for side, work in sides:
                @pl.when(side)
                def _():
                    for kind, group in work:
                        for c in group:
                            if kind != "recv":
                                c.wait_send()
                            if kind != "send":
                                c.wait_recv()

        started.append(finish)

    return [functools.partial(step, k) for k in range(bits + 1)]


def scatter_steps(bits, me, arrays, outs, arrived, h, mine, theirs, parts, held, send_sem, recv_sem):
    core = bits - 1
    orders = [order[::-1] for order in orders_of(bits, len(parts))]
    now = [[(ref, (part,)) for ref in arrays] for part in parts]
    dims = [list(range(bits + 1)) for _ in parts]
    copies = []

    def pick(p, d, value, tail):
        return (h, *(value if e == d else slice(None) for e in dims[p]), *tail)

    def send(p, k, a, src, dst, d):
        c = pltpu.make_async_remote_copy(
            src_ref=src, dst_ref=dst, send_sem=send_sem.at[p, k, a], recv_sem=recv_sem.at[p, k, a],
            device_id=partner_of(bits, me, d), device_id_type=MESH)
        c.start()
        copies.append(c)

    def step(k):
        ready = list(copies)
        copies.clear()
        if k > bits:
            for c in ready:
                c.wait()
            for a in range(2):
                outs[a][:, theirs] = arrived[a][h].astype(F32)
            return
        for p, part in enumerate(parts):
            for a in range(2):
                if k > 0:
                    d = orders[p][k - 1]
                    ready[2 * p + a].wait()
                    ref, tail = now[p][a]
                    slot = held[p][k - 1][a]
                    sums = ref[pick(p, d, me[d], tail)].astype(F32) + slot[h].astype(F32)
                    slot[h] = sums.astype(slot.dtype)
                    now[p][a] = (slot, (slice(None),))
                if k == bits:
                    outs[a][part, mine] = jnp.where(me[core] == 0, sums[0], sums[1])
                    send(p, k, a, slot.at[h, 1 - me[core]], arrived[a].at[h, part], core)
            if k > 0:
                dims[p].remove(orders[p][k - 1])
            if k < bits:
                d = orders[p][k]
                for a in range(2):
                    ref, tail = now[p][a]
                    send(p, k, a, ref.at[pick(p, d, 1 - me[d], tail)], held[p][k][a].at[h], d)

    return [functools.partial(step, k) for k in range(bits + 2)]


def layer_kernel(bits, sharing, q_ref, g_ref, k_ref, v_ref, o_ref, dq_ref, ok_ref, ov_ref,
                 ka, va, dka, dva, s_scr, p_scr, qin, gin, ost, dqst, qm, gm, om, dm, kst, vst, kin, vin,
                 ds_scr, qt, gt, qn, gn, acc, top, total, drow,
                 own_sem, pass_send, pass_recv, in_sem, swap_send, swap_recv, out_sem, back_send, back_recv,
                 lend_send, lend_recv, final_sem, gather_send, gather_recv, send_sem, recv_sem, *slots):
    rows, pair_width = k_ref.shape
    pairs = pair_width // HD
    heads = pairs // 2
    last = heads - 1
    core = bits - 1
    block = lax.axis_index("ctx")
    half = lax.axis_index("head") % 2
    span = 2 * rows
    wide = rows * sharing
    step_cols = 2 * rows
    scaling = 1.0 / math.sqrt(HD)
    factor = scaling * math.log2(math.e)
    me = my_bits(bits)
    slot_list = iter(slots)
    parts = pieces_of(rows)
    held = [[[next(slot_list) for _ in range(2)] for _ in range(bits)] for _ in parts]
    count = 2 ** bits
    light = block < count // 2
    beside = block + 1 - 2 * me[core]

    def columns(side, h, width):
        return pl.ds(pl.multiple_of((side * heads + h) * width, width), width)

    def local(src, dst, sem):
        return pltpu.make_async_copy(src, dst, sem)

    def remote(src, dst, send, recv, d):
        return pltpu.make_async_remote_copy(
            src_ref=src, dst_ref=dst, send_sem=send, recv_sem=recv,
            device_id=partner_of(bits, me, d), device_id_type=MESH)

    head_cols = sharing * HD
    pair_refs = ((k_ref, ka), (v_ref, va))
    row_refs = ((q_ref, qin), (g_ref, gin))
    out_refs = ((ost, o_ref), (dqst, dq_ref))
    own = [[local(src.at[:, columns(me[core], h, HD)], dst.at[(h, *me)], own_sem.at[h, a])
            for a, (src, dst) in enumerate(pair_refs)] for h in range(heads)]
    passed = [[remote(src.at[:, columns(1 - me[core], h, HD)], dst.at[(h, *me)], pass_send.at[h, a], pass_recv.at[h, a], core)
               for a, (src, dst) in enumerate(pair_refs)] for h in range(heads)]
    loads = [[local(src.at[:, columns(me[core], h, head_cols)], dst.at[0, h], in_sem.at[h, a])
              for a, (src, dst) in enumerate(row_refs)] for h in range(heads)]
    swaps = [[remote(src.at[:, columns(1 - me[core], h, head_cols)], dst.at[1, h], swap_send.at[h, a], swap_recv.at[h, a], core)
              for a, (src, dst) in enumerate(row_refs)] for h in range(heads)]
    stores = [[local(src.at[0, h], dst.at[:, columns(me[core], h, head_cols)], out_sem.at[h, a])
               for a, (src, dst) in enumerate(out_refs)] for h in range(heads)]
    backs = [[remote(src.at[1, h], dst.at[:, columns(me[core], h, head_cols)], back_send.at[h, a], back_recv.at[h, a], core)
              for a, (src, dst) in enumerate(out_refs)] for h in range(heads)]
    lend = [remote(src.at[:, columns(me[core], last, head_cols)], dst, lend_send.at[a], lend_recv.at[a], 0)
            for a, (src, dst) in enumerate(((q_ref, qm), (g_ref, gm)))]
    give = [remote(src, dst.at[:, columns(me[core], last, head_cols)], lend_send.at[2 + a], lend_recv.at[2 + a], 0)
            for a, (src, dst) in enumerate(((om, o_ref), (dm, dq_ref)))]

    def start(copies):
        for c in copies:
            c.start()

    def wait(copies):
        for c in copies:
            c.wait()

    for h in range(heads):
        start(own[h])
    start(loads[0])
    greet(bits, me)
    for h in range(heads):
        start(passed[h])
    start(swaps[0])

    @pl.when(light)
    def _():
        for h in range(1, heads):
            start(loads[h])

    @pl.when(~light)
    def _():
        start(lend)

    for h in range(1, heads):
        start(swaps[h])

    first_k = gather_steps(bits, me, light, (ka,), 0, last > 0, parts, gather_send.at[0], gather_recv.at[0])
    first_v = gather_steps(bits, me, light, (va,), 0, last > 0, parts, gather_send.at[1], gather_recv.at[1])
    rest = gather_steps(bits, me, light, (ka, va), slice(1, heads), False, parts, gather_send.at[2], gather_recv.at[2])

    def advance(work):
        if work:
            work.pop(0)()

    def drain(work):
        while work:
            work.pop(0)()

    def keys_at(b, many):
        return pl.ds(pl.multiple_of(b * span, span), many * span)

    def bits_of(b, many=1):
        ctx = tuple(b // 2 ** (bits - 1 - d) % 2 for d in range(bits))
        return ctx if many == 1 else ctx[:-1]

    def load(ref, g, b, many):
        return ref[(g, *bits_of(b, many))].reshape(many * span, HD)

    def each(first, stop, body):
        @pl.loop(0, stop // 2)
        def _(i):
            body(2 * i, 2)

        @pl.when(stop % 2 == 1)
        def _():
            body(stop - 1, 1)

    def clear(g, first):
        for ref in (dka, dva):
            @pl.loop(first, count)
            def _(b):
                ref[(g, *bits_of(b))] = jnp.zeros((2, rows, HD), ref.dtype)

    def prepare(q_src, g_src):
        for h in range(sharing):
            part = slice(h * rows, (h + 1) * rows)
            qt[:, part] = q_src[:, h * HD:(h + 1) * HD].T
            gt[:, part] = g_src[:, h * HD:(h + 1) * HD].T
        top[...] = jnp.full_like(top, -jnp.inf)

    def attend(g, block, out_ref, dq_out, again, polls):
        def poll():
            if polls:
                polls.pop(0)()

        def scores(b, many, masked=False):
            kb = load(ka, g, b, many)
            for c in range(0, wide, step_cols):
                cols = slice(c, c + step_cols)
                s = dot(kb, qt[:, cols])
                if masked:
                    key_pos = lax.broadcasted_iota(jnp.int32, s.shape, 0)
                    row_pos = half * rows + lax.broadcasted_iota(jnp.int32, s.shape, 1) % rows
                    s = jnp.where(key_pos <= row_pos, s, -jnp.inf)
                s_scr[keys_at(b, many), cols] = s
                top[:, cols] = jnp.maximum(top[:, cols], s.reshape(many * span // 8, 8, step_cols).max(axis=0))

        each(0, block, scores)
        scores(block, 1, True)
        poll()
        highest = jnp.max(top[...], axis=0, keepdims=True) * factor
        total[...] = jnp.zeros_like(total)
        acc[...] = jnp.zeros_like(acc)

        def weigh(b, many):
            vt = load(va, g, b, many).T
            for c in range(0, wide, step_cols):
                cols = slice(c, c + step_cols)
                p = jnp.exp2(s_scr[keys_at(b, many), cols] * factor - highest[:, cols])
                total[:, cols] += p.reshape(many * span // 8, 8, step_cols).sum(axis=0)
                pb = p.astype(BF16)
                p_scr[keys_at(b, many), cols] = pb
                acc[:, cols] += dot(vt, pb)

        each(0, block + 1, weigh)
        poll()
        inverse = 1.0 / jnp.sum(total[...], axis=0, keepdims=True)
        for h in range(sharing):
            part = slice(h * rows, (h + 1) * rows)
            inv = inverse[:, part]
            out = (acc[:, part] * inv).astype(BF16)
            out_ref[:, h * HD:(h + 1) * HD] = out.T
            grad = gt[:, part].astype(F32)
            drow[:, part] = jnp.sum(grad * out.astype(F32), axis=0, keepdims=True)
            gn[part, :] = (grad * inv).astype(BF16).T
            qn[part, :] = (qt[:, part].astype(F32) * (inv * scaling)).astype(BF16).T
        acc[...] = jnp.zeros_like(acc)

        def back(b, many):
            keys = slice(0, many * span)
            kt = load(ka, g, b, many).T
            vb = load(va, g, b, many)
            for c in range(0, wide, step_cols):
                cols = slice(c, c + step_cols)
                dp = dot(vb, gt[:, cols])
                pb = p_scr[keys_at(b, many), cols]
                ds_scr[keys, cols] = (pb.astype(F32) * (dp - drow[:, cols])).astype(BF16)
            dk = dot(ds_scr[keys, :], qn[...])
            dv = dot(p_scr[keys_at(b, many), :], gn[...])
            for c in range(0, wide, step_cols):
                cols = slice(c, c + step_cols)
                acc[:, cols] += dot(kt, ds_scr[keys, cols])
            for ref, add in ((dka, dk), (dva, dv)):
                where = (g, *bits_of(b, many))
                if again:
                    add = add + load(ref, g, b, many).astype(F32)
                ref[where] = add.astype(ref.dtype).reshape(ref[where].shape)

        each(0, block + 1, back)
        poll()
        for h in range(sharing):
            part = slice(h * rows, (h + 1) * rows)
            dq = (acc[:, part] * (inverse[:, part] * scaling)).astype(dq_out.dtype)
            dq_out[:, h * HD:(h + 1) * HD] = dq.T

    def scatter(h):
        return scatter_steps(bits, me, (dka, dva), (kst, vst), (kin, vin), h, columns(me[core], h, HD),
                             columns(1 - me[core], h, HD), parts, held, send_sem.at[h], recv_sem.at[h])

    wait(own[0])
    wait(passed[0])
    advance(first_k)
    advance(first_v)
    wait(loads[0])
    prepare(qin.at[0, 0], gin.at[0, 0])
    for h in range(last):
        clear(h, block + 1)
    clear(last, jnp.where(light, block + count // 2 + 1, 0))
    advance(first_k)
    advance(first_v)
    for h in range(1, heads):
        wait(own[h])
        wait(passed[h])
    advance(rest)
    for k in range(2, bits):
        advance(first_k)
        advance(first_v)
        advance(rest)
    drain(first_k)

    pending = []
    for h in range(last):
        polls = [lambda: drain(first_v), lambda: advance(rest), lambda: None]
        if h > 0:
            drain(rest)
            wait(loads[h])
            prepare(qin.at[0, h], gin.at[0, h])
            polls = []
        attend(h, block, ost.at[0, h], dqst.at[0, h], False, polls)
        start(stores[h])
        wait(swaps[h])
        prepare(qin.at[1, h], gin.at[1, h])
        attend(h, beside, ost.at[1, h], dqst.at[1, h], True, [])
        start(backs[h])
        work = scatter(h)
        advance(work)
        pending.append(work)
    drain(rest)
    wait(swaps[last])

    @pl.when(light)
    def _():
        for c in lend:
            c.wait_recv()
        prepare(qm, gm)
        attend(last, block + count // 2, om, dm, False, [])
        start(give)
        wait(loads[last])
        prepare(qin.at[0, last], gin.at[0, last])
        attend(last, block, ost.at[0, last], dqst.at[0, last], True, [])
        start(stores[last])

    def step():
        for work in pending:
            advance(work)

    prepare(qin.at[1, last], gin.at[1, last])
    attend(last, beside, ost.at[1, last], dqst.at[1, last], True, [])
    start(backs[last])
    pending.insert(0, scatter(last))
    while any(pending):
        step()
    finals = [local(src, dst, final_sem.at[a]) for a, (src, dst) in enumerate(((kst, ok_ref), (vst, ov_ref)))]
    start(finals)

    @pl.when(light)
    def _():
        wait(stores[last])
        for c in give:
            c.wait_send()

    @pl.when(~light)
    def _():
        for c in lend:
            c.wait_send()
        for c in give:
            c.wait_recv()

    for h in range(last):
        wait(stores[h])
    for h in range(heads):
        wait(backs[h])
    wait(finals)


def layer(bits, q, g, k, v):
    rows, width = q.shape
    pair_width = k.shape[1]
    pairs = pair_width // HD
    sharing = width // pair_width
    wide = rows * sharing
    seq = 2 ** (bits + 1) * rows
    heads = pairs // 2
    parts = pieces_of(rows)
    count = len(parts)
    anyspace = pl.BlockSpec(memory_space=pl.ANY)
    whole = pltpu.VMEM((heads,) + (2,) * (bits + 1) + (rows, HD), BF16)
    sem = pltpu.SemaphoreType.DMA
    slots = [pltpu.VMEM((heads,) + (2,) * (bits - k) + (part.stop - part.start, HD), BF16)
             for part in parts for k in range(bits) for _ in range(2)]
    head = (rows, sharing * HD)
    return pl.pallas_call(
        functools.partial(layer_kernel, bits, sharing),
        out_shape=(
            jax.ShapeDtypeStruct((rows, width), BF16),
            jax.ShapeDtypeStruct((rows, width), BF16),
            jax.ShapeDtypeStruct((rows, pair_width), F32),
            jax.ShapeDtypeStruct((rows, pair_width), F32),
        ),
        in_specs=[anyspace] * 4,
        out_specs=(anyspace,) * 4,
        scratch_shapes=[
            whole, whole, whole, whole,
            pltpu.VMEM((seq, wide), F32),
            pltpu.VMEM((seq, wide), BF16),
            *[pltpu.VMEM((2, heads) + head, BF16) for _ in range(4)],
            *[pltpu.VMEM(head, BF16) for _ in range(4)],
            *[pltpu.VMEM((rows, pair_width), F32) for _ in range(2)],
            *[pltpu.VMEM((heads, rows, HD), BF16) for _ in range(2)],
            pltpu.VMEM((4 * rows, wide), BF16),
            *[pltpu.VMEM((HD, wide), BF16) for _ in range(2)],
            *[pltpu.VMEM((wide, HD), BF16) for _ in range(2)],
            pltpu.VMEM((HD, wide), F32),
            pltpu.VMEM((8, wide), F32),
            pltpu.VMEM((8, wide), F32),
            pltpu.VMEM((1, wide), F32),
            *[sem((heads, 2)) for _ in range(9)],
            sem((4,)),
            sem((4,)),
            sem((2,)),
            *[sem((3, count, bits, 2)) for _ in range(2)],
            *[sem((heads, count, bits + 1, 2)) for _ in range(2)],
        ] + slots,
        compiler_params=pltpu.CompilerParams(collective_id=0, has_side_effects=True, vmem_limit_bytes=63 * 2**20),
        name="layer",
    )(q, g, k, v)


def widen_kernel(o_in, dq_in, k_in, v_in, o_out, dq_out, k_out, v_out):
    o_out[...] = o_in[...]
    dq_out[...] = dq_in[...].astype(dq_out.dtype)
    k_out[...] = k_in[...]
    v_out[...] = v_in[...]


def widen(arrays, dtypes):
    rows = arrays[0].shape[0]
    tile = rows // 2
    specs = [pl.BlockSpec((tile, x.shape[1]), lambda i: (i, 0)) for x in arrays]
    return pl.pallas_call(
        widen_kernel,
        out_shape=tuple(jax.ShapeDtypeStruct(x.shape, t) for x, t in zip(arrays, dtypes)),
        grid=(rows // tile,),
        in_specs=specs,
        out_specs=tuple(specs),
        name="widen",
    )(*arrays)


def on_device(query_input, key_input, value_input, grad_input):
    bits = (lax.axis_size("ctx") - 1).bit_length()
    outs = layer(bits, query_input[0], grad_input[0], key_input[0], value_input[0])
    outs = widen(outs, (BF16, F32, F32, F32))
    return tuple(out[None] for out in outs)


def solution(mesh):
    spec = P("ctx", "head", None)
    return jax.shard_map(on_device, mesh=mesh, in_specs=(spec,) * 4, out_specs=(spec,) * 4, check_vma=False)
```

```python
import functools
import math

import jax
import jax.numpy as jnp
from jax import lax
from jax.experimental import pallas as pl
from jax.experimental.pallas import tpu as pltpu
from jax.sharding import PartitionSpec as P

HD = 128
NN = (((1,), (0,)), ((), ()))
F32 = jnp.float32
BF16 = jnp.bfloat16
MESH = pl.DeviceIdType.MESH


def dot(a, b, dims=NN):
    return lax.dot_general(a, b, dims, preferred_element_type=F32)


def pieces_of(size):
    unit = 16
    units = size // unit
    count = min(3, units)
    sizes = [(units // count + (1 if i < units % count else 0)) * unit for i in range(count)]
    starts = [sum(sizes[:i]) for i in range(count)]
    return [slice(a, a + s) for a, s in zip(starts, sizes)]


def orders_of(bits, count):
    links = [d for d in range(bits + 1) if d != bits - 1]
    return [[links[(i + p) % len(links)] for i in range(len(links))] for p in range(count)]


def my_bits(bits):
    block = lax.axis_index("ctx")
    return [block // 2 ** (bits - 1 - d) % 2 for d in range(bits)] + [lax.axis_index("head") % 2]


def partner_of(bits, me, d):
    if d == bits:
        return {"head": lax.axis_index("head") + 1 - 2 * me[d]}
    return {"ctx": lax.axis_index("ctx") + (1 - 2 * me[d]) * 2 ** (bits - 1 - d)}


def greet(bits, me):
    barrier = pltpu.get_barrier_semaphore()
    for d in range(bits + 1):
        pl.semaphore_signal(barrier, inc=1, device_id=partner_of(bits, me, d), device_id_type=MESH)
    pl.semaphore_wait(barrier, bits + 1)


def gather_steps(bits, me, light, arrays, heads, causal, parts, send_sem, recv_sem):
    orders = orders_of(bits, len(parts))
    started = []

    def copies_at(p, k, top):
        region = list(me)
        region[bits - 1] = slice(None)
        for d in orders[p][:k]:
            region[d] = slice(None)
        if not top:
            region[0] = me[0]
        index = (heads, *region, parts[p])
        return [pltpu.make_async_remote_copy(
            src_ref=ref.at[index], dst_ref=ref.at[index],
            send_sem=send_sem.at[p, k, a], recv_sem=recv_sem.at[p, k, a],
            device_id=partner_of(bits, me, orders[p][k]), device_id_type=MESH) for a, ref in enumerate(arrays)]

    def step(k):
        for act in started:
            act()
        started.clear()
        if k == bits:
            return
        low, high = [], []
        for p in range(len(parts)):
            done = orders[p][:k]
            full = copies_at(p, k, True)
            if causal and orders[p][k] == 0:
                low.append(("send", full))
                high.append(("recv", full))
            elif causal and 0 in done:
                low.append(("both", copies_at(p, k, False)))
                high.append(("both", full))
            else:
                for c in full:
                    c.start()
                low.append(("wait", full))
                high.append(("wait", full))
        sides = ((light, low), (~light, high))
        for side, work in sides:
            sent = [c for kind, group in work if kind in ("send", "both") for c in group]
            if sent:
                @pl.when(side)
                def _():
                    for c in sent:
                        c.start()

        def finish():
            if all(kind == "wait" for kind, _ in low):
                for _, group in low:
                    for c in group:
                        c.wait()
                return
            for side, work in sides:
                @pl.when(side)
                def _():
                    for kind, group in work:
                        for c in group:
                            if kind != "recv":
                                c.wait_send()
                            if kind != "send":
                                c.wait_recv()

        started.append(finish)

    return [functools.partial(step, k) for k in range(bits + 1)]


def scatter_steps(bits, me, arrays, outs, arrived, h, mine, theirs, parts, held, send_sem, recv_sem):
    core = bits - 1
    orders = [order[::-1] for order in orders_of(bits, len(parts))]
    now = [[(ref, (part,)) for ref in arrays] for part in parts]
    dims = [list(range(bits + 1)) for _ in parts]
    copies = []

    def pick(p, d, value, tail):
        return (h, *(value if e == d else slice(None) for e in dims[p]), *tail)

    def send(p, k, a, src, dst, d):
        c = pltpu.make_async_remote_copy(
            src_ref=src, dst_ref=dst, send_sem=send_sem.at[p, k, a], recv_sem=recv_sem.at[p, k, a],
            device_id=partner_of(bits, me, d), device_id_type=MESH)
        c.start()
        copies.append(c)

    def step(k):
        ready = list(copies)
        copies.clear()
        if k > bits:
            for c in ready:
                c.wait()
            for a in range(2):
                outs[a][:, theirs] = arrived[a][h].astype(F32)
            return
        for p, part in enumerate(parts):
            for a in range(2):
                if k > 0:
                    d = orders[p][k - 1]
                    ready[2 * p + a].wait()
                    ref, tail = now[p][a]
                    slot = held[p][k - 1][a]
                    sums = ref[pick(p, d, me[d], tail)].astype(F32) + slot[h].astype(F32)
                    slot[h] = sums.astype(slot.dtype)
                    now[p][a] = (slot, (slice(None),))
                if k == bits:
                    outs[a][part, mine] = jnp.where(me[core] == 0, sums[0], sums[1])
                    send(p, k, a, slot.at[h, 1 - me[core]], arrived[a].at[h, part], core)
            if k > 0:
                dims[p].remove(orders[p][k - 1])
            if k < bits:
                d = orders[p][k]
                for a in range(2):
                    ref, tail = now[p][a]
                    send(p, k, a, ref.at[pick(p, d, 1 - me[d], tail)], held[p][k][a].at[h], d)

    return [functools.partial(step, k) for k in range(bits + 2)]


def layer_kernel(bits, sharing, q_ref, g_ref, k_ref, v_ref, o_ref, dq_ref, ok_ref, ov_ref,
                 ka, va, dka, dva, s_scr, p_scr, qin, gin, ost, dqst, qm, gm, om, dm, kst, vst, kin, vin,
                 ds_scr, qt, gt, qn, gn, acc, top, total, drow,
                 own_sem, pass_send, pass_recv, in_sem, swap_send, swap_recv, out_sem, back_send, back_recv,
                 lend_send, lend_recv, final_sem, gather_send, gather_recv, send_sem, recv_sem, *slots):
    rows, pair_width = k_ref.shape
    pairs = pair_width // HD
    heads = pairs // 2
    last = heads - 1
    core = bits - 1
    block = lax.axis_index("ctx")
    half = lax.axis_index("head") % 2
    span = 2 * rows
    wide = rows * sharing
    step_cols = 2 * rows
    scaling = 1.0 / math.sqrt(HD)
    factor = scaling * math.log2(math.e)
    me = my_bits(bits)
    slot_list = iter(slots)
    parts = pieces_of(rows)
    held = [[[next(slot_list) for _ in range(2)] for _ in range(bits)] for _ in parts]
    count = 2 ** bits
    light = block < count // 2
    beside = block + 1 - 2 * me[core]

    def columns(side, h, width):
        return pl.ds(pl.multiple_of((side * heads + h) * width, width), width)

    def local(src, dst, sem):
        return pltpu.make_async_copy(src, dst, sem)

    def remote(src, dst, send, recv, d):
        return pltpu.make_async_remote_copy(
            src_ref=src, dst_ref=dst, send_sem=send, recv_sem=recv,
            device_id=partner_of(bits, me, d), device_id_type=MESH)

    head_cols = sharing * HD
    pair_refs = ((k_ref, ka), (v_ref, va))
    row_refs = ((q_ref, qin), (g_ref, gin))
    out_refs = ((ost, o_ref), (dqst, dq_ref))
    own = [[local(src.at[:, columns(me[core], h, HD)], dst.at[(h, *me)], own_sem.at[h, a])
            for a, (src, dst) in enumerate(pair_refs)] for h in range(heads)]
    passed = [[remote(src.at[:, columns(1 - me[core], h, HD)], dst.at[(h, *me)], pass_send.at[h, a], pass_recv.at[h, a], core)
               for a, (src, dst) in enumerate(pair_refs)] for h in range(heads)]
    loads = [[local(src.at[:, columns(me[core], h, head_cols)], dst.at[0, h], in_sem.at[h, a])
              for a, (src, dst) in enumerate(row_refs)] for h in range(heads)]
    swaps = [[remote(src.at[:, columns(1 - me[core], h, head_cols)], dst.at[1, h], swap_send.at[h, a], swap_recv.at[h, a], core)
              for a, (src, dst) in enumerate(row_refs)] for h in range(heads)]
    stores = [[local(src.at[0, h], dst.at[:, columns(me[core], h, head_cols)], out_sem.at[h, a])
               for a, (src, dst) in enumerate(out_refs)] for h in range(heads)]
    backs = [[remote(src.at[1, h], dst.at[:, columns(me[core], h, head_cols)], back_send.at[h, a], back_recv.at[h, a], core)
              for a, (src, dst) in enumerate(out_refs)] for h in range(heads)]
    lend = [remote(src.at[:, columns(me[core], last, head_cols)], dst, lend_send.at[a], lend_recv.at[a], 0)
            for a, (src, dst) in enumerate(((q_ref, qm), (g_ref, gm)))]
    give = [remote(src, dst.at[:, columns(me[core], last, head_cols)], lend_send.at[2 + a], lend_recv.at[2 + a], 0)
            for a, (src, dst) in enumerate(((om, o_ref), (dm, dq_ref)))]

    def start(copies):
        for c in copies:
            c.start()

    def wait(copies):
        for c in copies:
            c.wait()

    for h in range(heads):
        start(own[h])
    start(loads[0])
    greet(bits, me)
    for h in range(heads):
        start(passed[h])
    start(swaps[0])

    @pl.when(light)
    def _():
        for h in range(1, heads):
            start(loads[h])

    @pl.when(~light)
    def _():
        start(lend)

    for h in range(1, heads):
        start(swaps[h])

    first_k = gather_steps(bits, me, light, (ka,), 0, last > 0, parts, gather_send.at[0], gather_recv.at[0])
    first_v = gather_steps(bits, me, light, (va,), 0, last > 0, parts, gather_send.at[1], gather_recv.at[1])
    rest = gather_steps(bits, me, light, (ka, va), slice(1, heads), False, parts, gather_send.at[2], gather_recv.at[2])

    def advance(work):
        if work:
            work.pop(0)()

    def drain(work):
        while work:
            work.pop(0)()

    def keys_at(b, many):
        return pl.ds(pl.multiple_of(b * span, span), many * span)

    def bits_of(b, many=1):
        ctx = tuple(b // 2 ** (bits - 1 - d) % 2 for d in range(bits))
        return ctx[:bits - many.bit_length() + 1]

    def load(ref, g, b, many):
        return ref[(g, *bits_of(b, many))].reshape(many * span, HD)

    def each(first, stop, body):
        @pl.loop(0, stop // 2)
        def _(i):
            body(2 * i, 2)

        single(stop, body)

    def each_four(stop, body):
        @pl.loop(0, stop // 4)
        def _(i):
            body(4 * i, 4)

        @pl.when(stop // 2 % 2 == 1)
        def _():
            body(stop // 4 * 4, 2)

        single(stop, body)

    def single(stop, body):
        @pl.when(stop % 2 == 1)
        def _():
            body(stop - 1, 1)

    def clear(g, first):
        for ref in (dka, dva):
            @pl.loop(first, count)
            def _(b):
                ref[(g, *bits_of(b))] = jnp.zeros((2, rows, HD), ref.dtype)

    def prepare(q_src, g_src):
        for h in range(sharing):
            part = slice(h * rows, (h + 1) * rows)
            qt[:, part] = q_src[:, h * HD:(h + 1) * HD].T
            gt[:, part] = g_src[:, h * HD:(h + 1) * HD].T
        top[...] = jnp.full_like(top, -jnp.inf)

    def attend(g, block, out_ref, dq_out, again, polls):
        def poll():
            if polls:
                polls.pop(0)()

        def scores(b, many, masked=False):
            kb = load(ka, g, b, many)
            for c in range(0, wide, step_cols):
                cols = slice(c, c + step_cols)
                s = dot(kb, qt[:, cols])
                if masked:
                    key_pos = lax.broadcasted_iota(jnp.int32, s.shape, 0)
                    row_pos = half * rows + lax.broadcasted_iota(jnp.int32, s.shape, 1) % rows
                    s = jnp.where(key_pos <= row_pos, s, -jnp.inf)
                s_scr[keys_at(b, many), cols] = s
                top[:, cols] = jnp.maximum(top[:, cols], s.reshape(many * span // 8, 8, step_cols).max(axis=0))

        each_four(block, scores)
        scores(block, 1, True)
        poll()
        highest = jnp.max(top[...], axis=0, keepdims=True) * factor
        total[...] = jnp.zeros_like(total)
        acc[...] = jnp.zeros_like(acc)

        def weigh(b, many):
            vt = load(va, g, b, many).T
            for c in range(0, wide, step_cols):
                cols = slice(c, c + step_cols)
                p = jnp.exp2(s_scr[keys_at(b, many), cols] * factor - highest[:, cols])
                total[:, cols] += p.reshape(many * span // 8, 8, step_cols).sum(axis=0)
                pb = p.astype(BF16)
                p_scr[keys_at(b, many), cols] = pb
                acc[:, cols] += dot(vt, pb)

        each_four(block + 1, weigh)
        poll()
        inverse = 1.0 / jnp.sum(total[...], axis=0, keepdims=True)
        for h in range(sharing):
            part = slice(h * rows, (h + 1) * rows)
            inv = inverse[:, part]
            out = (acc[:, part] * inv).astype(BF16)
            out_ref[:, h * HD:(h + 1) * HD] = out.T
            grad = gt[:, part].astype(F32)
            drow[:, part] = jnp.sum(grad * out.astype(F32), axis=0, keepdims=True)
            gn[part, :] = (grad * inv).astype(BF16).T
            qn[part, :] = (qt[:, part].astype(F32) * (inv * scaling)).astype(BF16).T
        acc[...] = jnp.zeros_like(acc)

        def back(b, many):
            keys = slice(0, many * span)
            kt = load(ka, g, b, many).T
            vb = load(va, g, b, many)
            for c in range(0, wide, step_cols):
                cols = slice(c, c + step_cols)
                dp = dot(vb, gt[:, cols])
                pb = p_scr[keys_at(b, many), cols]
                ds_scr[keys, cols] = (pb.astype(F32) * (dp - drow[:, cols])).astype(BF16)
            dk = dot(ds_scr[keys, :], qn[...])
            dv = dot(p_scr[keys_at(b, many), :], gn[...])
            for c in range(0, wide, step_cols):
                cols = slice(c, c + step_cols)
                acc[:, cols] += dot(kt, ds_scr[keys, cols])
            for ref, add in ((dka, dk), (dva, dv)):
                where = (g, *bits_of(b, many))
                if again:
                    add = add + load(ref, g, b, many).astype(F32)
                ref[where] = add.astype(ref.dtype).reshape(ref[where].shape)

        each(0, block + 1, back)
        poll()
        for h in range(sharing):
            part = slice(h * rows, (h + 1) * rows)
            dq = (acc[:, part] * (inverse[:, part] * scaling)).astype(dq_out.dtype)
            dq_out[:, h * HD:(h + 1) * HD] = dq.T

    def scatter(h):
        return scatter_steps(bits, me, (dka, dva), (kst, vst), (kin, vin), h, columns(me[core], h, HD),
                             columns(1 - me[core], h, HD), parts, held, send_sem.at[h], recv_sem.at[h])

    wait(own[0])
    wait(passed[0])
    advance(first_k)
    advance(first_v)
    wait(loads[0])
    prepare(qin.at[0, 0], gin.at[0, 0])
    for h in range(last):
        clear(h, block + 1)
    clear(last, jnp.where(light, block + count // 2 + 1, 0))
    advance(first_k)
    advance(first_v)
    for h in range(1, heads):
        wait(own[h])
        wait(passed[h])
    advance(rest)
    for k in range(2, bits):
        advance(first_k)
        advance(first_v)
        advance(rest)
    drain(first_k)

    pending = []
    for h in range(last):
        polls = [lambda: drain(first_v), lambda: advance(rest), lambda: None]
        if h > 0:
            drain(rest)
            wait(loads[h])
            prepare(qin.at[0, h], gin.at[0, h])
            polls = []
        attend(h, block, ost.at[0, h], dqst.at[0, h], False, polls)
        start(stores[h])
        wait(swaps[h])
        prepare(qin.at[1, h], gin.at[1, h])
        attend(h, beside, ost.at[1, h], dqst.at[1, h], True, [])
        start(backs[h])
        work = scatter(h)
        advance(work)
        pending.append(work)
    drain(rest)
    wait(swaps[last])

    @pl.when(light)
    def _():
        for c in lend:
            c.wait_recv()
        prepare(qm, gm)
        attend(last, block + count // 2, om, dm, False, [])
        start(give)
        wait(loads[last])
        prepare(qin.at[0, last], gin.at[0, last])
        attend(last, block, ost.at[0, last], dqst.at[0, last], True, [])
        start(stores[last])

    def step():
        for work in pending:
            advance(work)

    prepare(qin.at[1, last], gin.at[1, last])
    attend(last, beside, ost.at[1, last], dqst.at[1, last], True, [])
    start(backs[last])
    pending.insert(0, scatter(last))
    while any(pending):
        step()
    finals = [local(src, dst, final_sem.at[a]) for a, (src, dst) in enumerate(((kst, ok_ref), (vst, ov_ref)))]
    start(finals)

    @pl.when(light)
    def _():
        wait(stores[last])
        for c in give:
            c.wait_send()

    @pl.when(~light)
    def _():
        for c in lend:
            c.wait_send()
        for c in give:
            c.wait_recv()

    for h in range(last):
        wait(stores[h])
    for h in range(heads):
        wait(backs[h])
    wait(finals)


def layer(bits, q, g, k, v):
    rows, width = q.shape
    pair_width = k.shape[1]
    pairs = pair_width // HD
    sharing = width // pair_width
    wide = rows * sharing
    seq = 2 ** (bits + 1) * rows
    heads = pairs // 2
    parts = pieces_of(rows)
    count = len(parts)
    anyspace = pl.BlockSpec(memory_space=pl.ANY)
    whole = pltpu.VMEM((heads,) + (2,) * (bits + 1) + (rows, HD), BF16)
    sem = pltpu.SemaphoreType.DMA
    slots = [pltpu.VMEM((heads,) + (2,) * (bits - k) + (part.stop - part.start, HD), BF16)
             for part in parts for k in range(bits) for _ in range(2)]
    head = (rows, sharing * HD)
    return pl.pallas_call(
        functools.partial(layer_kernel, bits, sharing),
        out_shape=(
            jax.ShapeDtypeStruct((rows, width), BF16),
            jax.ShapeDtypeStruct((rows, width), BF16),
            jax.ShapeDtypeStruct((rows, pair_width), F32),
            jax.ShapeDtypeStruct((rows, pair_width), F32),
        ),
        in_specs=[anyspace] * 4,
        out_specs=(anyspace,) * 4,
        scratch_shapes=[
            whole, whole, whole, whole,
            pltpu.VMEM((seq, wide), F32),
            pltpu.VMEM((seq, wide), BF16),
            *[pltpu.VMEM((2, heads) + head, BF16) for _ in range(4)],
            *[pltpu.VMEM(head, BF16) for _ in range(4)],
            *[pltpu.VMEM((rows, pair_width), F32) for _ in range(2)],
            *[pltpu.VMEM((heads, rows, HD), BF16) for _ in range(2)],
            pltpu.VMEM((4 * rows, wide), BF16),
            *[pltpu.VMEM((HD, wide), BF16) for _ in range(2)],
            *[pltpu.VMEM((wide, HD), BF16) for _ in range(2)],
            pltpu.VMEM((HD, wide), F32),
            pltpu.VMEM((8, wide), F32),
            pltpu.VMEM((8, wide), F32),
            pltpu.VMEM((1, wide), F32),
            *[sem((heads, 2)) for _ in range(9)],
            sem((4,)),
            sem((4,)),
            sem((2,)),
            *[sem((3, count, bits, 2)) for _ in range(2)],
            *[sem((heads, count, bits + 1, 2)) for _ in range(2)],
        ] + slots,
        compiler_params=pltpu.CompilerParams(collective_id=0, has_side_effects=True, vmem_limit_bytes=63 * 2**20),
        name="layer",
    )(q, g, k, v)


def widen_kernel(o_in, dq_in, k_in, v_in, o_out, dq_out, k_out, v_out):
    o_out[...] = o_in[...]
    dq_out[...] = dq_in[...].astype(dq_out.dtype)
    k_out[...] = k_in[...]
    v_out[...] = v_in[...]


def widen(arrays, dtypes):
    rows = arrays[0].shape[0]
    tile = rows // 2
    specs = [pl.BlockSpec((tile, x.shape[1]), lambda i: (i, 0)) for x in arrays]
    return pl.pallas_call(
        widen_kernel,
        out_shape=tuple(jax.ShapeDtypeStruct(x.shape, t) for x, t in zip(arrays, dtypes)),
        grid=(rows // tile,),
        in_specs=specs,
        out_specs=tuple(specs),
        name="widen",
    )(*arrays)


def on_device(query_input, key_input, value_input, grad_input):
    bits = (lax.axis_size("ctx") - 1).bit_length()
    outs = layer(bits, query_input[0], grad_input[0], key_input[0], value_input[0])
    outs = widen(outs, (BF16, F32, F32, F32))
    return tuple(out[None] for out in outs)


def solution(mesh):
    spec = P("ctx", "head", None)
    return jax.shard_map(on_device, mesh=mesh, in_specs=(spec,) * 4, out_specs=(spec,) * 4, check_vma=False)
```
